128 devices in a mesh: tensor: 8 (over z, core), fsdp: 16 (over x, y).
Axes of the slice: x: 4, y: 4, z: 4, core: 2. Of those that a mesh axis runs over, the one named last changes fastest.
Arguments:
- momentum: float32 [4096, 28672], P('tensor', 'fsdp'), may hold values from -6 to 6
- gradient: bfloat16 [4096, 28672], P('tensor', 'fsdp'), may hold values from -6 to 6
- right_factor: float32 [28672, 512], P('fsdp'), may hold values from -0.03125 to 0.03125
Outputs:
- new_momentum: float32 [4096, 28672], P('tensor', 'fsdp')
- update: float32 [4096, 28672], P('tensor', 'fsdp')
- new_right: float32 [28672, 512], P('fsdp')
The draws below stay inside these ranges and needn't reach their ends.
All inputs are finite; a program needn't handle non-finite values.
Results may differ from the reference program's by a relative error of at most 0.0003.
Values sent between devices are 32-bit elements; how exact they have to be, the bound alone decides.
A program may use at most 128 MiB of HBM per device.

```python
import jax
import jax.numpy as jnp
from jax import lax

ROWS = 4096
COLS = 28672
RANK = 512


def shard_levels(rng, extent, pieces, least, top_value):
    level, own = 1.0, jax.random.fold_in(rng, 6)
    for dim, blocks in pieces:
        draws = jnp.exp(jax.random.uniform(jax.random.fold_in(own, dim), (blocks,), jnp.float32, least / len(pieces), top_value / len(pieces)))
        level = level * jnp.repeat(draws, extent[dim] // blocks).reshape([-1 if axis == dim else 1 for axis in range(len(extent))])
    return level


def centred(stream_key, dims, deviation, reach, split=(), dtype=jnp.bfloat16):
    level = shard_levels(stream_key, dims, split, -0.22, 0.18) if split else 1.0
    result = jax.random.normal(stream_key, dims, jnp.float32) * deviation * level
    return jnp.minimum(jnp.maximum(result, -reach), reach).astype(dtype)


def setup_inputs(seed: int = 0) -> dict:
    splits = jax.random.split(jax.random.key(seed), 4)
    return {
        "momentum": centred(splits[0], (ROWS, COLS), 1.0, 6.0, ((0, 8), (1, 16)), jnp.float32),
        "gradient": centred(splits[1], (ROWS, COLS), 1.0, 6.0, ((0, 8), (1, 16))),
        "right_factor": centred(splits[2], (COLS, RANK), COLS ** -0.5, 0.03125, ((0, 16),), jnp.float32),
    }


def inner_rows(first, second):
    return lax.dot_general(first.astype(jnp.float32), second.astype(jnp.float32), (((0,), (0,)), ((), ())), precision=lax.Precision.HIGHEST, preferred_element_type=jnp.float32)

def outer_rank(first, second):
    return lax.dot_general(first.astype(jnp.float32), second.astype(jnp.float32), (((1,), (1,)), ((), ())), precision=lax.Precision.HIGHEST, preferred_element_type=jnp.float32)

def reference(momentum, gradient, right_factor):
    buffer = momentum + gradient.astype(jnp.float32)
    left = jnp.dot(buffer.astype(jnp.float32), right_factor.astype(jnp.float32), precision=lax.Precision.HIGHEST, preferred_element_type=jnp.float32)
    gram = inner_rows(left, left)
    lower = jnp.linalg.cholesky(gram)
    ortho = jax.scipy.linalg.solve_triangular(lower, left.T, lower=True).T
    right = inner_rows(buffer, ortho)
    new_momentum = buffer - 0.05 * outer_rank(ortho, right)
    colsq = lax.optimization_barrier(jnp.sum(right * right, axis=0))
    new_right = right / jnp.sqrt(colsq + 1e-06)
    scale = jnp.sqrt(jnp.float32(ROWS * COLS / RANK))
    update = scale * outer_rank(ortho, new_right)
    return (new_momentum, update, new_right)
```

```python
import functools

import jax
import jax.numpy as jnp
from jax import lax
from jax.experimental import pallas as pl
from jax.experimental.pallas import tpu as pltpu
from jax.sharding import Mesh
from jax.sharding import PartitionSpec as P

ROWS = 4096
COLS = 28672
RANK = 512
FSDP = ("fsdp_0", "fsdp_1")
TENSOR = ("tensor_0", "tensor_1")
R = 512
N = 1792
B = 32
MESH = pl.DeviceIdType.MESH
HIGHEST = lax.Precision.HIGHEST
F32 = jnp.float32
BF16 = jnp.bfloat16


def mul(a, b, dims=((1,), (0,)), precision=None):
    return lax.dot_general(a, b, (dims, ((), ())), precision=precision, preferred_element_type=F32)


def halves(x):
    high = x.astype(BF16)
    return high, (x - high.astype(F32)).astype(BF16)


def mul3(ah, al, bh, bl, dims=((1,), (0,))):
    return mul(ah, bh, dims) + (mul(ah, bl, dims) + mul(al, bh, dims))


def factor(block, off):
    n = B // 8
    row = lax.broadcasted_iota(jnp.int32, (8, 128), 0)
    lane = lax.broadcasted_iota(jnp.int32, (8, 128), 1)
    spread = functools.partial(jnp.broadcast_to, shape=(8, 128))
    col = [[None if h < m // 8 else spread(block[8 * h : 8 * h + 8, off + m : off + m + 1]) for h in range(n)] for m in range(B)]
    inv = [(row + 8 * h == lane).astype(F32) for h in range(n)]
    for j in range(B):
        g, s = j // 8, j % 8
        r = lax.rsqrt(spread(col[j][g][s : s + 1, :]))
        low = [None if h < g else col[j][h] * r for h in range(n)]
        top = spread(inv[g][s : s + 1, :]) * r
        inv[g] = jnp.where(row == s, top, inv[g])
        if s < 7:
            inv[g] = inv[g] - jnp.where(row > s, low[g], 0.0) * top
        for h in range(g + 1, n):
            inv[h] = inv[h] - low[h] * top
        for m in range(j + 1, B):
            u = spread(low[m // 8][m % 8 : m % 8 + 1, :])
            for h in range(m // 8, n):
                col[m][h] = col[m][h] - low[h] * u
    return jnp.concatenate(inv, axis=0)


def cholesky_step(aug, k):
    r0 = k * B
    r1 = r0 + B
    lo = 128 * (r0 // 128)
    hi = R + lo + 128
    t = factor(aug[r0:r1, lo : lo + 128], r0 - lo)[:, :B]
    u = mul(t, aug[r0:r1, lo:hi], precision=HIGHEST)
    aug[r0:r1, R:hi] = u[:, R - lo :]
    over_rows = ((0,), (0,))
    if r1 < R:
        r2 = r1 + B
        aug[r1:r2, lo:hi] = aug[r1:r2, lo:hi] - mul(u[:, r1 - lo : r2 - lo], u, over_rows, HIGHEST)
        if r2 < R:
            aug[r2:, lo:hi] = aug[r2:, lo:hi] - mul(u[:, r2 - lo : R - lo], u, over_rows, HIGHEST)


def work(
    mom_ref, grad_ref, rf_ref,
    rt_out, om_ref, odh_ref, odl_ref, d_ref,
    mom, grad, rf, bh, bl, rh, rl, lp, left, rsb, ltf, lth, ltl,
    wp, wo, wr, z1, z2, wf, gsend, grecv, gz, gg, aug, rt, csb,
    in_sem, out_sem,
    ls_send, ls_recv, la_send, la_recv,
    g_send, g_recv, ga_send, ga_recv, gc_send, gc_recv,
    wc_send, wc_recv, wz_send, wz_recv, wd_send, wd_recv,
    cs_send, cs_recv,
):
    z, c = lax.axis_index("tensor_0"), lax.axis_index("tensor_1")
    x, y = lax.axis_index("fsdp_0"), lax.axis_index("fsdp_1")
    other_core = {"tensor_1": 1 - c}

    def one(i):
        return i + 1 - 2 * lax.rem(i, 2), lax.rem(lax.rem(i, 2) + lax.div(i, 2), 2)

    def two(i):
        return 3 - i, lax.div(i, 2)

    (xa, xab), (xb, xbb) = one(x), two(x)
    (ya, yab), (yb, ybb) = one(y), two(y)
    (za, zab), (zb, zbb) = one(z), two(z)
    plane = [({"fsdp_0": xa}, xab), ({"fsdp_1": ya}, yab), ({"fsdp_0": xb}, xbb), ({"fsdp_1": yb}, ybb)]
    orders = [plane[p:] + plane[:p] for p in range(4)]
    column = [({"tensor_0": za}, zab), ({"tensor_0": zb}, zbb)]
    zorders = [[column[q % 2], column[1 - q % 2]] for q in range(4)]

    def rows(start, size):
        return pl.ds(pl.multiple_of(start, 8), size)

    def send(src, dst, send_sem, recv_sem, to):
        copy = pltpu.make_async_remote_copy(src, dst, send_sem, recv_sem, device_id=to, device_id_type=MESH)
        copy.start()
        sent.append(copy)
        return copy

    sent = []

    barrier = pltpu.get_barrier_semaphore()
    plane_peers = [(lax.rem(x + dx, 4), lax.rem(y + dy, 4)) for dx in range(4) for dy in range(4) if dx or dy]
    z_peers = [lax.rem(z + dz, 4) for dz in range(1, 4)]
    for px, py in plane_peers:
        pl.semaphore_signal(barrier, inc=1, device_id={"fsdp_0": px, "fsdp_1": py}, device_id_type=MESH)
    for pz in z_peers:
        pl.semaphore_signal(barrier, inc=1, device_id={"tensor_0": pz}, device_id_type=MESH)
    pl.semaphore_signal(barrier, inc=1, device_id=other_core, device_id_type=MESH)

    ins = []
    for i in range(4):
        s = slice(448 * i, 448 * i + 448)
        ins.append(pltpu.make_async_copy(rf_ref.at[s], rf.at[s], in_sem.at[i]))
    for i in range(2):
        s = slice(256 * i, 256 * i + 256)
        ins.append(pltpu.make_async_copy(mom_ref.at[s], mom.at[s], in_sem.at[4 + i]))
        ins.append(pltpu.make_async_copy(grad_ref.at[s], grad.at[s], in_sem.at[6 + i]))
    for copy in ins:
        copy.start()
    for i in range(4):
        s = slice(448 * i, 448 * i + 448)
        ins[i].wait()
        rh[s, :], rl[s, :] = halves(rf[s, :])

    off = [[128 * p] for p in range(4)]
    for p in range(4):
        for s in range(4):
            off[p].append(off[p][s] + orders[p][s][1] * (64 >> s))
    start_row = [0, 64, 96, 112]
    scatter = [[None] * 4 for _ in range(4)]

    def scatter_send(p, s):
        to, bit = orders[p][s]
        size = 64 >> s
        src = lp.at[rows(off[p][s] + (1 - bit) * size, size)]
        dst = rsb.at[p, start_row[s] : start_row[s] + size]
        scatter[p][s] = send(src, dst, ls_send.at[p, s], ls_recv.at[p, s], to)

    for i in range(2):
        s = slice(256 * i, 256 * i + 256)
        ins[4 + 2 * i].wait()
        ins[5 + 2 * i].wait()
        bh[s, :], bl[s, :] = halves(mom[s, :] + grad[s, :].astype(F32))
        lp[s, :] = mul3(bh[s, :], bl[s, :], rh[...], rl[...])
        if i == 0:
            pl.semaphore_wait(barrier, 19)
        for p in (2 * i, 2 * i + 1):
            scatter_send(p, 0)
    gather = [[None] * 4 for _ in range(4)]

    def gather_send(p, s):
        to, _ = orders[p][s]
        part = left.at[rows(off[p][s + 1], 64 >> s)]
        gather[p][s] = send(part, part, la_send.at[p, s], la_recv.at[p, s], to)

    for s in range(4):
        size = 64 >> s
        for p in range(4):
            scatter[p][s].wait_recv()
            keep = rows(off[p][s + 1], size)
            total = lp[keep, :] + rsb[p, start_row[s] : start_row[s] + size, :]
            if s < 3:
                lp[keep, :] = total
                scatter_send(p, s + 1)
            else:
                left[keep, :] = total
                gather_send(p, 3)
    for s in (3, 2, 1, 0):
        for p in range(4):
            gather[p][s].wait_recv()
            if s:
                gather_send(p, s - 1)

    ltf[...] = left[...].T
    goff = [[256 * c] for p in range(4)]
    for p in range(4):
        for s in range(4):
            goff[p].append(goff[p][s] + orders[p][s][1] * (128 >> s))
    for p in range(4):
        block = left[:, 128 * p : 128 * p + 128]
        rel = goff[p][4] - 256 * c
        gsend[p] = mul(ltf[rows(rel + 256 * (1 - c), 16), :], block, precision=HIGHEST)
    gram_core = send(gsend, grecv, g_send.at[0], g_recv.at[0], other_core)
    gown = []
    for p in range(4):
        block = left[:, 128 * p : 128 * p + 128]
        gown.append(mul(ltf[rows(goff[p][4], 16), :], block, precision=HIGHEST))
    gram_z = []

    def gram_1():
        gram_core.wait_recv()
        for p in range(4):
            gz[z, p] = gown[p] + grecv[p]
        for i, pz in enumerate(z_peers):
            gram_z.append(send(gz.at[z], gz.at[z], g_send.at[1 + i], g_recv.at[1 + i], {"tensor_0": pz}))

    gram_gather = [[None] * 4 for _ in range(4)]

    def gram_send(p, s):
        to, _ = orders[p][s]
        part = gg.at[p, rows(goff[p][s + 1], 128 >> s)]
        gram_gather[p][s] = send(part, part, ga_send.at[p, s], ga_recv.at[p, s], to)

    def gram_2():
        for copy in gram_z:
            copy.wait_recv()
        for p in range(4):
            gg[p, rows(goff[p][4], 16), :] = (gz[0, p] + gz[1, p]) + (gz[2, p] + gz[3, p])
            gram_send(p, 3)

    def gram_3(s):
        for p in range(4):
            gram_gather[p][s].wait_recv()
            if s:
                gram_send(p, s - 1)
            else:
                part = gg.at[p, rows(256 * c, 256)]
                gram_gather[p][0] = send(part, part, gc_send.at[p], gc_recv.at[p], other_core)

    def gram_4():
        for p in range(4):
            gram_gather[p][0].wait_recv()
            aug[:, 128 * p : 128 * p + 128] = gg[p]
        row = lax.broadcasted_iota(jnp.int32, (R, R), 0)
        aug[:, R:] = (row == lax.broadcasted_iota(jnp.int32, (R, R), 1)).astype(F32)

    lth[...], ltl[...] = halves(ltf[...])
    wcore = [None] * 4
    wscatter = [[None, None] for _ in range(4)]
    wgather = [[None, None, None] for _ in range(4)]

    def w_other(i):
        s = rows(256 * (1 - c) + 128 * i, 128)
        wp[128 * i : 128 * i + 128, :] = mul3(lth[s, :], ltl[s, :], bh[...], bl[...])
        for q in (2 * i, 2 * i + 1):
            part = slice(64 * q, 64 * q + 64)
            wcore[q] = send(wp.at[part], wr.at[part], wc_send.at[q], wc_recv.at[q], other_core)

    def w_own(i):
        s = rows(256 * c + 128 * i, 128)
        wo[128 * i : 128 * i + 128, :] = mul3(lth[s, :], ltl[s, :], bh[...], bl[...])

    woff = []
    for q in range(4):
        o1 = 64 * q + 32 * zorders[q][0][1]
        woff.append((64 * q, o1, o1 + 16 * zorders[q][1][1]))

    def w_send(q, s, buf):
        to, bit = zorders[q][s]
        size = 32 >> s
        src = wo.at[rows(woff[q][s] + (1 - bit) * size, size)]
        wscatter[q][s] = send(src, buf.at[q], wz_send.at[q, s], wz_recv.at[q, s], to)

    def w_1(q):
        wcore[q].wait_recv()
        part = slice(64 * q, 64 * q + 64)
        wo[part, :] = wo[part, :] + wr[part, :]
        w_send(q, 0, z1)

    def w_2(q):
        wscatter[q][0].wait_recv()
        keep = rows(woff[q][1], 32)
        wo[keep, :] = wo[keep, :] + z1[q]
        w_send(q, 1, z2)

    def w_gather(q, i, start, size, to):
        part = wf.at[rows(256 * c + start, size)]
        wgather[q][i] = send(part, part, wd_send.at[q, i], wd_recv.at[q, i], to)

    def w_3(q):
        wscatter[q][1].wait_recv()
        wf[rows(256 * c + woff[q][2], 16), :] = wo[rows(woff[q][2], 16), :] + z2[q]
        w_gather(q, 0, woff[q][2], 16, zorders[q][1][0])

    def w_4(q):
        wgather[q][0].wait_recv()
        w_gather(q, 1, woff[q][1], 32, zorders[q][0][0])

    def w_5(q):
        wgather[q][1].wait_recv()
        w_gather(q, 2, woff[q][0], 64, other_core)

    w_other(0)
    gram_1()
    w_other(1)
    gram_2()
    w_own(0)
    gram_3(3)
    w_1(0)
    w_1(1)
    w_own(1)
    gram_3(2)
    w_1(2)
    w_1(3)
    gram_3(1)
    w_2(0)
    w_2(1)
    gram_3(0)
    gram_4()
    between = {
        0: [(w_2, 2), (w_2, 3)],
        2: [(w_3, 0), (w_3, 1)],
        4: [(w_3, 2), (w_3, 3)],
        6: [(w_4, 0), (w_4, 1)],
        8: [(w_4, 2), (w_4, 3)],
        11: [(w_5, 0), (w_5, 1)],
        15: [(w_5, 2), (w_5, 3)],
    }
    for k in range(R // B):
        cholesky_step(aug, k)
        for step, q in between.get(k, []):
            step(q)

    for q in range(4):
        wgather[q][2].wait_recv()
    for i in range(2):
        depth = 256 * i + 256
        ih, il = halves(aug[256 * i : depth, R : R + depth])
        for n in range(0, N, 256):
            wh, wl = halves(wf[:depth, n : n + 256])
            rt[256 * i : depth, n : n + 256] = mul3(ih, il, wh, wl)
    out = pltpu.make_async_copy(rt, rt_out, out_sem)
    out.start()

    me = 4 * x + y
    sums = jnp.zeros((R, 128), F32)
    for n in range(0, N, 128):
        sums = sums + rt[:, n : n + 128] * rt[:, n : n + 128]
    line = [jnp.sum(sums[128 * i : 128 * i + 128].T, axis=0, keepdims=True) for i in range(4)]
    csb[me] = jnp.concatenate(line + [jnp.zeros((4, 128), F32)], axis=0)
    squares = []
    for i, (px, py) in enumerate(plane_peers):
        to = {"fsdp_0": px, "fsdp_1": py}
        squares.append(send(csb.at[me], csb.at[me], cs_send.at[i], cs_recv.at[i], to))
    lh, ll = halves(left[...])
    ih, il = halves(aug[:, R:])
    ortho = mul3(lh, ll, ih, il, ((1,), (1,)))
    om_ref[...] = (ortho * 0.05).astype(BF16)
    for copy in squares:
        copy.wait_recv()
    total = csb[0]
    for i in range(1, 16):
        total = total + csb[i]
    norm = 1.0 / jnp.sqrt(total + 1e-06)
    d = jnp.concatenate([norm[i : i + 1, :] for i in range(4)], axis=1)
    d_ref[...] = jnp.broadcast_to(d, (8, R))
    scale = (ROWS * COLS / RANK) ** 0.5
    odh_ref[...], odl_ref[...] = halves(ortho * (d * scale))
    out.wait()
    for copy in sent:
        copy.wait_send()


def finish(mom, grad, rt, om, odh, odl, d, new_mom, update, new_right):
    right = rt[...]
    rh, rl = halves(right)
    new_mom[...] = mom[...] + grad[...].astype(F32) - mul(om[...], rh)
    update[...] = mul3(odh[...], odl[...], rh, rl)
    new_right[...] = right.T * d[0:1, :]


def per_device(momentum, gradient, right_factor):
    vmem, dma, anywhere = pltpu.VMEM, pltpu.SemaphoreType.DMA, pl.BlockSpec(memory_space=pl.ANY)
    inside = pl.BlockSpec(memory_space=pltpu.VMEM)
    rt, om, odh, odl, d = pl.pallas_call(
        work,
        out_shape=[
            jax.ShapeDtypeStruct((R, N), F32),
            jax.ShapeDtypeStruct((R, RANK), BF16),
            jax.ShapeDtypeStruct((R, RANK), BF16),
            jax.ShapeDtypeStruct((R, RANK), BF16),
            jax.ShapeDtypeStruct((8, RANK), F32),
        ],
        in_specs=[anywhere] * 3,
        out_specs=[anywhere, inside, inside, inside, inside],
        scratch_shapes=[
            vmem((R, N), F32), vmem((R, N), BF16), vmem((N, RANK), F32),
            vmem((R, N), BF16), vmem((R, N), BF16), vmem((N, RANK), BF16), vmem((N, RANK), BF16),
            vmem((R, RANK), F32), vmem((R, RANK), F32), vmem((4, 120, RANK), F32),
            vmem((RANK, R), F32), vmem((RANK, R), BF16), vmem((RANK, R), BF16),
            vmem((256, N), F32), vmem((256, N), F32), vmem((256, N), F32),
            vmem((4, 32, N), F32), vmem((4, 16, N), F32), vmem((RANK, N), F32),
            vmem((4, 16, 128), F32), vmem((4, 16, 128), F32), vmem((4, 4, 16, 128), F32), vmem((4, RANK, 128), F32),
            vmem((RANK, 2 * RANK), F32), vmem((RANK, N), F32), vmem((16, 8, 128), F32),
            dma((8,)), dma,
            dma((4, 4)), dma((4, 4)), dma((4, 4)), dma((4, 4)),
            dma((4,)), dma((4,)), dma((4, 4)), dma((4, 4)), dma((4,)), dma((4,)),
            dma((4,)), dma((4,)), dma((4, 2)), dma((4, 2)), dma((4, 3)), dma((4, 3)),
            dma((15,)), dma((15,)),
        ],
        compiler_params=pltpu.CompilerParams(
            collective_id=0, has_side_effects=True, vmem_limit_bytes=62 << 20
        ),
        name="dion",
    )(momentum, gradient, right_factor)
    wide = 256
    tall = pl.BlockSpec((R, wide), lambda i: (0, i))
    whole = pl.BlockSpec((R, RANK), lambda i: (0, 0))
    return pl.pallas_call(
        finish,
        out_shape=[
            jax.ShapeDtypeStruct((R, N), F32),
            jax.ShapeDtypeStruct((R, N), F32),
            jax.ShapeDtypeStruct((N, RANK), F32),
        ],
        grid=(N // wide,),
        in_specs=[tall, tall, tall, whole, whole, whole, pl.BlockSpec((8, RANK), lambda i: (0, 0))],
        out_specs=[tall, tall, pl.BlockSpec((wide, RANK), lambda i: (i, 0))],
        name="finish",
    )(momentum, gradient, rt, om, odh, odl, d)


def solution(mesh):
    finer = Mesh(mesh.devices.reshape(4, 2, 4, 4), ("tensor_0", "tensor_1", "fsdp_0", "fsdp_1"))
    placed = (P(TENSOR, FSDP), P(TENSOR, FSDP), P(FSDP, None))
    return jax.shard_map(
        per_device,
        mesh=finer,
        in_specs=placed,
        out_specs=(P(TENSOR, FSDP), P(TENSOR, FSDP), P(FSDP, None)),
        check_vma=False,
    )
```

```python
import functools

import jax
import jax.numpy as jnp
from jax import lax
from jax.experimental import pallas as pl
from jax.experimental.pallas import tpu as pltpu
from jax.sharding import Mesh
from jax.sharding import PartitionSpec as P

ROWS = 4096
COLS = 28672
RANK = 512
FSDP = ("fsdp_0", "fsdp_1")
TENSOR = ("tensor_0", "tensor_1")
R = 512
N = 1792
B = 32
MESH = pl.DeviceIdType.MESH
HIGHEST = lax.Precision.HIGHEST
F32 = jnp.float32
BF16 = jnp.bfloat16
NT = ((1,), (1,))


def mul(a, b, dims=((1,), (0,)), precision=None):
    return lax.dot_general(a, b, (dims, ((), ())), precision=precision, preferred_element_type=F32)


def halves(x):
    high = x.astype(BF16)
    return high, (x - high.astype(F32)).astype(BF16)


def mul3(ah, al, bh, bl, dims=((1,), (0,))):
    return mul(ah, bh, dims) + (mul(ah, bl, dims) + mul(al, bh, dims))


def thirds(x):
    high = x.astype(BF16)
    rest = x - high.astype(F32)
    middle = rest.astype(BF16)
    return high, middle, (rest - middle.astype(F32)).astype(BF16)


def spread(x):
    return jnp.broadcast_to(x, (8, 128))


def factor(block, off):
    n = B // 8
    row = lax.broadcasted_iota(jnp.int32, (8, 128), 0)
    lane = lax.broadcasted_iota(jnp.int32, (8, 128), 1) % B
    rest = [block[8 * h : 8 * h + 8] for h in range(n)]
    inv = [(row + 8 * h == lane).astype(F32) for h in range(n)]
    for base in range(0, B, 16):
        end = base + 16
        col = {m: {h: spread(rest[h][:, off + m : off + m + 1]) for h in range(m // 8, n)} for m in range(base, end)}
        for j in range(base, end):
            g, s = j // 8, j % 8
            r = lax.rsqrt(spread(col[j][g][s : s + 1, :]))
            low = {h: col[j][h] * r for h in range(g, n)}
            top = spread(inv[g][s : s + 1, :]) * r
            inv[g] = jnp.where(row == s, top, inv[g])
            if s < 7:
                inv[g] = inv[g] - jnp.where(row > s, low[g], 0.0) * top
            for h in range(g + 1, n):
                inv[h] = inv[h] - low[h] * top
            for m in range(j + 1, end):
                u = spread(low[m // 8][m % 8 : m % 8 + 1, :])
                for h in range(m // 8, n):
                    col[m][h] = col[m][h] - low[h] * u
            if end < B:
                line = spread(rest[g][s : s + 1, :]) * r
                for h in range(g, n):
                    rest[h] = rest[h] - low[h] * line
    return jnp.concatenate(inv, axis=0)


def paired(x):
    high, middle, low = (part.astype(F32) for part in thirds(x))
    place = lax.broadcasted_iota(jnp.int32, x.shape, 1) // B
    first = jnp.where(place % 2 == 0, high, middle).astype(BF16)
    return first, jnp.where(place == 0, low, high).astype(BF16)[:, : 2 * B]


def stacked(x):
    high, middle, low = thirds(x)
    return jnp.concatenate([high, high, middle, middle], axis=0), jnp.concatenate([high, low], axis=0)


def six(first, second):
    return mul(first[0], second[0]) + mul(first[1], second[1])


def cholesky_step(aug, k):
    r0 = k * B
    r1 = r0 + B
    lo = 128 * (r0 // 128)
    hi = R + lo + 128
    off = r0 - lo
    t = factor(aug[r0:r1, lo : lo + 128], off)
    u = six(paired(t), stacked(aug[r0:r1, lo:hi]))
    aug[r0:r1, R:hi] = u[:, R - lo :]
    if r1 == R:
        return
    high, middle, low = thirds(u)
    over = jnp.concatenate([high, middle, high, middle, low, high], axis=0)
    under = jnp.concatenate([high, high, middle, middle, high, low], axis=0)
    top = r1
    while top < R:
        left = 128 * (top // 128)
        end = r1 + B if top == r1 else left + 128
        if end > top:
            part = mul(over[:, top - lo : end - lo], under[:, left - lo :], ((0,), (0,)))
            aug[top:end, left:hi] = aug[top:end, left:hi] - part
        top = end


def work(
    mom_ref, grad_ref, rf_ref,
    rt_out, om_ref, odh_ref, odl_ref, d_ref,
    mom, grad, rf, bh, bl, rh, rl, lp, left, rsb, ltf, lth, ltl,
    wp, wo, wr, z1, z2, wf, gs, gz, gq, aug, rt, csb,
    in_sem, out_sem,
    ls_send, ls_recv, la_send, la_recv,
    g_send, g_recv, ga_send, ga_recv, gc_send, gc_recv,
    wc_send, wc_recv, wz_send, wz_recv, wd_send, wd_recv,
    cs_send, cs_recv,
):
    z, c = lax.axis_index("tensor_0"), lax.axis_index("tensor_1")
    x, y = lax.axis_index("fsdp_0"), lax.axis_index("fsdp_1")
    me = 4 * x + y
    other_core = {"tensor_1": 1 - c}

    def one(i):
        return i + 1 - 2 * lax.rem(i, 2), lax.rem(lax.rem(i, 2) + lax.div(i, 2), 2)

    def two(i):
        return 3 - i, lax.div(i, 2)

    (xa, xab), (xb, xbb) = one(x), two(x)
    (ya, yab), (yb, ybb) = one(y), two(y)
    (za, zab), (zb, zbb) = one(z), two(z)
    plane = [({"fsdp_0": xa}, xab), ({"fsdp_1": ya}, yab), ({"fsdp_0": xb}, xbb), ({"fsdp_1": yb}, ybb)]
    orders = [plane[p:] + plane[:p] for p in range(4)]
    column = [({"tensor_0": za}, zab), ({"tensor_0": zb}, zbb)]
    zorders = [[column[q % 2], column[1 - q % 2]] for q in range(8)]

    def rows(start, size):
        return pl.ds(pl.multiple_of(start, 8), size)

    def send(src, dst, send_sem, recv_sem, to):
        copy = pltpu.make_async_remote_copy(src, dst, send_sem, recv_sem, device_id=to, device_id_type=MESH)
        copy.start()
        sent.append(copy)
        return copy

    sent = []

    barrier = pltpu.get_barrier_semaphore()
    plane_peers = [
        {"fsdp_0": lax.rem(x + dx, 4), "fsdp_1": lax.rem(y + dy, 4)} for dx in range(4) for dy in range(4) if dx or dy
    ]
    tensor_peers = [
        ({"tensor_0": lax.rem(z + dz, 4), "tensor_1": core}, core)
        for dz in range(4)
        for core in ((c, 1 - c) if dz else (1 - c,))
    ]
    for to in plane_peers + [to for to, _ in tensor_peers]:
        pl.semaphore_signal(barrier, inc=1, device_id=to, device_id_type=MESH)

    cuts = [(0, 512), (512, 1024), (1024, 1536), (1536, N)]
    ins = [[] for _ in range(4)]
    for i, (start, end) in enumerate(cuts):
        s = slice(start, end)
        ins[i].append(pltpu.make_async_copy(rf_ref.at[s], rf.at[s], in_sem.at[3 * i]))
        ins[i].append(pltpu.make_async_copy(mom_ref.at[:, s], mom.at[:, s], in_sem.at[3 * i + 1]))
        ins[i].append(pltpu.make_async_copy(grad_ref.at[:, s], grad.at[:, s], in_sem.at[3 * i + 2]))
    for piece in ins:
        for copy in piece:
            copy.start()

    scatter, gather = {}, {}
    flips = [(1, 0), (0, 1), (1, 1)]

    def quarter(p, stage):
        (to0, bit0), (to1, bit1) = orders[p][2 * stage : 2 * stage + 2]
        peers = []
        for f0, f1 in flips:
            to = {**(to0 if f0 else {}), **(to1 if f1 else {})}
            peers.append((to, 2 * (1 - bit0 if f0 else bit0) + (1 - bit1 if f1 else bit1)))
        return 2 * bit0 + bit1, peers

    quarters = [[quarter(p, stage) for stage in range(2)] for p in range(4)]
    large = [128 * p + 32 * quarters[p][0][0] for p in range(4)]
    small = [large[p] + 8 * quarters[p][1][0] for p in range(4)]

    def scatter_send(h, p, stage):
        base, size, place = (128 * p, 32, 0) if stage == 0 else (large[p], 8, 96)
        for i, (to, index) in enumerate(quarters[p][stage][1]):
            k = 3 * stage + i
            dst = rsb.at[h, p, place + size * i : place + size * i + size]
            src = lp.at[h, rows(base + size * index, size)]
            scatter[h, p, k] = send(src, dst, ls_send.at[h, p, k], ls_recv.at[h, p, k], to)

    def gather_send(h, p, stage):
        part = left.at[h, rows(small[p], 8) if stage else rows(large[p], 32)]
        for i, (to, _) in enumerate(quarters[p][stage][1]):
            k = 3 * stage + i
            gather[h, p, k] = send(part, part, la_send.at[h, p, k], la_recv.at[h, p, k], to)

    def left_step(h, i):
        for p in range(4):
            stage = i if i < 2 else 3 - i
            copies = gather if i >= 2 else scatter
            for k in range(3 * stage, 3 * stage + 3):
                copies[h, p, k].wait_recv()
            if i == 0:
                keep = rows(large[p], 32)
                lp[h, keep, :] = (lp[h, keep, :] + rsb[h, p, :32, :]) + (rsb[h, p, 32:64, :] + rsb[h, p, 64:96, :])
                scatter_send(h, p, 1)
            elif i == 1:
                keep = rows(small[p], 8)
                left[h, keep, :] = (lp[h, keep, :] + rsb[h, p, 96:104, :]) + (rsb[h, p, 104:112, :] + rsb[h, p, 112:, :])
                gather_send(h, p, 1)
            elif i == 2:
                gather_send(h, p, 0)

    for i, (start, end) in enumerate(cuts):
        for copy in ins[i]:
            copy.wait()
        s = slice(start, end)
        rh[s, :], rl[s, :] = halves(rf[s, :])
        bh[:, s], bl[:, s] = halves(mom[:, s] + grad[:, s].astype(F32))
        part = mul3(bh[:, s], bl[:, s], rh[s, :256], rl[s, :256])
        lp[0] = part if i == 0 else lp[0] + part
    pl.semaphore_wait(barrier, 22)
    for p in range(4):
        scatter_send(0, p, 0)
    lp[1] = mul3(bh[...], bl[...], rh[:, 256:], rl[:, 256:])
    for p in range(4):
        scatter_send(1, p, 0)

    places = [[(0, 0), (0, 1), (0, 2), (0, 3), (3, 3)], [(1, 1), (1, 2), (1, 3), (2, 2), (2, 3)]]
    grams = []

    def gram_1():
        mine = jnp.concatenate([ltf[rows(128 * t + 8 * me, 8), :] for t in range(4)], axis=0)
        part = [mul(mine, left[h], precision=HIGHEST) for h in range(2)]
        for core in range(2):
            for i, (t, n) in enumerate(places[core]):
                gs[core, i] = part[n // 2][8 * t : 8 * t + 8, 128 * (n % 2) : 128 * (n % 2) + 128]
        slot = 2 * z + c
        for i, (to, core) in enumerate(tensor_peers):
            grams.append(send(gs.at[core], gz.at[slot], g_send.at[i], g_recv.at[i], to))
        gz[slot] = gs[c]

    gathers = []

    def gram_2():
        for copy in grams:
            copy.wait_recv()
        total = gz[0]
        for i in range(1, 8):
            total = total + gz[i]
        gq[c, me] = total
        for i, to in enumerate(plane_peers):
            part = gq.at[c, me]
            gathers.append(send(part, part, ga_send.at[i], ga_recv.at[i], to))

    def gram_3():
        for copy in gathers:
            copy.wait_recv()
        grams.append(send(gq.at[c], gq.at[c], gc_send, gc_recv, other_core))

    def gram_4():
        grams[-1].wait_recv()
        for core in range(2):
            for i, (t, n) in enumerate(places[core]):
                for j in range(16):
                    aug[128 * t + 8 * j : 128 * t + 8 * j + 8, 128 * n : 128 * n + 128] = gq[core, j, i]
        row = lax.broadcasted_iota(jnp.int32, (R, R), 0)
        aug[:, R:] = (row == lax.broadcasted_iota(jnp.int32, (R, R), 1)).astype(F32)

    wcore, wscatter, wgather = {}, {}, {}

    def turn(h):
        half = slice(256 * h, 256 * h + 256)
        ltf[half, :] = left[h].T
        lth[half, :], ltl[half, :] = halves(ltf[half, :])

    def w_other(h):
        s = rows(256 * h + 128 * (1 - c), 128)
        wp[h] = mul3(lth[s, :], ltl[s, :], bh[...], bl[...])
        for q in range(4):
            part = slice(32 * q, 32 * q + 32)
            k = 4 * h + q
            wcore[k] = send(wp.at[h, part], wr.at[h, part], wc_send.at[k], wc_recv.at[k], other_core)

    def w_own(h):
        s = rows(256 * h + 128 * c, 128)
        wo[h] = mul3(lth[s, :], ltl[s, :], bh[...], bl[...])

    woff = []
    for q in range(8):
        o0 = 32 * (q % 4)
        o1 = o0 + 16 * zorders[q][0][1]
        woff.append((o0, o1, o1 + 8 * zorders[q][1][1]))

    def w_send(q, s, buf):
        to, bit = zorders[q][s]
        size = 16 >> s
        src = wo.at[q // 4, rows(woff[q][s] + (1 - bit) * size, size)]
        wscatter[q, s] = send(src, buf.at[q], wz_send.at[q, s], wz_recv.at[q, s], to)

    def w_1(q):
        wcore[q].wait_recv()
        part = slice(woff[q][0], woff[q][0] + 32)
        wo[q // 4, part, :] = wo[q // 4, part, :] + wr[q // 4, part, :]
        w_send(q, 0, z1)

    def w_2(q):
        wscatter[q, 0].wait_recv()
        keep = rows(woff[q][1], 16)
        wo[q // 4, keep, :] = wo[q // 4, keep, :] + z1[q]
        w_send(q, 1, z2)

    def w_gather(q, i, start, size, to):
        part = wf.at[rows(256 * (q // 4) + 128 * c + start, size)]
        wgather[q, i] = send(part, part, wd_send.at[q, i], wd_recv.at[q, i], to)

    def w_3(q):
        wscatter[q, 1].wait_recv()
        own = rows(256 * (q // 4) + 128 * c + woff[q][2], 8)
        wf[own, :] = wo[q // 4, rows(woff[q][2], 8), :] + z2[q]
        w_gather(q, 0, woff[q][2], 8, zorders[q][1][0])

    def w_4(q):
        wgather[q, 0].wait_recv()
        w_gather(q, 1, woff[q][1], 16, zorders[q][0][0])

    def w_5(q):
        wgather[q, 1].wait_recv()
        w_gather(q, 2, woff[q][0], 32, other_core)

    def pairs(step, *firsts):
        return [(step, q) for first in firsts for q in (first, first + 1)]

    for i in range(3):
        left_step(0, i)
        left_step(1, i)
    left_step(0, 3)
    turn(0)
    w_other(0)
    left_step(1, 3)
    turn(1)
    gram_1()
    w_own(0)
    for step, q in pairs(w_1, 0, 2):
        step(q)
    w_other(1)
    w_own(1)
    for step, q in pairs(w_1, 4, 6):
        step(q)
    gram_2()
    for step, q in pairs(w_2, 0, 2):
        step(q)
    gram_3()
    gram_4()
    for step, q in pairs(w_2, 4, 6):
        step(q)
    between = {
        0: pairs(w_3, 0, 2),
        2: pairs(w_3, 4, 6),
        4: pairs(w_4, 0, 2),
        6: pairs(w_4, 4, 6),
        10: pairs(w_5, 0, 2),
        15: pairs(w_5, 4, 6),
    }
    for k in range(R // B):
        cholesky_step(aug, k)
        for step, q in between.get(k, []):
            step(q)

    for q in range(4):
        wgather[q, 2].wait_recv()
    ih, il = halves(aug[:, R : R + 256])
    for n in range(0, N, 256):
        wh, wl = halves(wf[:256, n : n + 256])
        rt[:, n : n + 256] = mul3(ih, il, wh, wl)
    for q in range(4, 8):
        wgather[q, 2].wait_recv()
    ih, il = halves(aug[256:, R + 256 :])
    for n in range(0, N, 256):
        wh, wl = halves(wf[256:, n : n + 256])
        rt[256:, n : n + 256] = rt[256:, n : n + 256] + mul3(ih, il, wh, wl)
    out = pltpu.make_async_copy(rt, rt_out, out_sem)
    out.start()

    sums = jnp.zeros((R, 128), F32)
    for n in range(0, N, 128):
        sums = sums + rt[:, n : n + 128] * rt[:, n : n + 128]
    line = [jnp.sum(sums[128 * i : 128 * i + 128].T, axis=0, keepdims=True) for i in range(4)]
    csb[me] = jnp.concatenate(line + [jnp.zeros((4, 128), F32)], axis=0)
    squares = []
    for i, to in enumerate(plane_peers):
        squares.append(send(csb.at[me], csb.at[me], cs_send.at[i], cs_recv.at[i], to))
    lh, ll = halves(jnp.concatenate([left[0], left[1]], axis=1))
    ih, il = halves(aug[:, R:])
    ortho = mul3(lh, ll, ih, il, NT)
    om_ref[...] = (ortho * 0.05).astype(BF16)
    for copy in squares:
        copy.wait_recv()
    total = csb[0]
    for i in range(1, 16):
        total = total + csb[i]
    norm = 1.0 / jnp.sqrt(total + 1e-06)
    d = jnp.concatenate([norm[i : i + 1, :] for i in range(4)], axis=1)
    d_ref[...] = jnp.broadcast_to(d, (8, R))
    scale = (ROWS * COLS / RANK) ** 0.5
    odh_ref[...], odl_ref[...] = halves(ortho * (d * scale))
    out.wait()
    for copy in sent:
        copy.wait_send()


def finish(mom, grad, rt, om, odh, odl, d, new_mom, update, new_right):
    right = rt[...]
    rh, rl = halves(right)
    new_mom[...] = mom[...] + grad[...].astype(F32) - mul(om[...], rh)
    update[...] = mul3(odh[...], odl[...], rh, rl)
    new_right[...] = right.T * d[0:1, :]


def per_device(momentum, gradient, right_factor):
    vmem, dma, anywhere = pltpu.VMEM, pltpu.SemaphoreType.DMA, pl.BlockSpec(memory_space=pl.ANY)
    inside = pl.BlockSpec(memory_space=pltpu.VMEM)
    rt, om, odh, odl, d = pl.pallas_call(
        work,
        out_shape=[
            jax.ShapeDtypeStruct((R, N), F32),
            jax.ShapeDtypeStruct((R, RANK), BF16),
            jax.ShapeDtypeStruct((R, RANK), BF16),
            jax.ShapeDtypeStruct((R, RANK), BF16),
            jax.ShapeDtypeStruct((8, RANK), F32),
        ],
        in_specs=[anywhere] * 3,
        out_specs=[anywhere, inside, inside, inside, inside],
        scratch_shapes=[
            vmem((R, N), F32), vmem((R, N), BF16), vmem((N, RANK), F32),
            vmem((R, N), BF16), vmem((R, N), BF16), vmem((N, RANK), BF16), vmem((N, RANK), BF16),
            vmem((2, R, 256), F32), vmem((2, R, 256), F32), vmem((2, 4, 120, 256), F32),
            vmem((RANK, R), F32), vmem((RANK, R), BF16), vmem((RANK, R), BF16),
            vmem((2, 128, N), F32), vmem((2, 128, N), F32), vmem((2, 128, N), F32),
            vmem((8, 16, N), F32), vmem((8, 8, N), F32), vmem((RANK, N), F32),
            vmem((2, 5, 8, 128), F32), vmem((8, 5, 8, 128), F32), vmem((2, 16, 5, 8, 128), F32),
            vmem((RANK, 2 * RANK), F32), vmem((RANK, N), F32), vmem((16, 8, 128), F32),
            dma((12,)), dma,
            dma((2, 4, 6)), dma((2, 4, 6)), dma((2, 4, 6)), dma((2, 4, 6)),
            dma((7,)), dma((7,)), dma((15,)), dma((15,)), dma, dma,
            dma((8,)), dma((8,)), dma((8, 2)), dma((8, 2)), dma((8, 3)), dma((8, 3)),
            dma((15,)), dma((15,)),
        ],
        compiler_params=pltpu.CompilerParams(
            collective_id=0, has_side_effects=True, vmem_limit_bytes=62 << 20
        ),
        name="dion",
    )(momentum, gradient, right_factor)
    wide = 896
    tall = pl.BlockSpec((R, wide), lambda i: (0, i))
    whole = pl.BlockSpec((R, RANK), lambda i: (0, 0))
    return pl.pallas_call(
        finish,
        out_shape=[
            jax.ShapeDtypeStruct((R, N), F32),
            jax.ShapeDtypeStruct((R, N), F32),
            jax.ShapeDtypeStruct((N, RANK), F32),
        ],
        grid=(N // wide,),
        in_specs=[tall, tall, tall, whole, whole, whole, pl.BlockSpec((8, RANK), lambda i: (0, 0))],
        out_specs=[tall, tall, pl.BlockSpec((wide, RANK), lambda i: (i, 0))],
        compiler_params=pltpu.CompilerParams(vmem_limit_bytes=56 << 20),
        name="finish",
    )(momentum, gradient, rt, om, odh, odl, d)


def solution(mesh):
    finer = Mesh(mesh.devices.reshape(4, 2, 4, 4), ("tensor_0", "tensor_1", "fsdp_0", "fsdp_1"))
    placed = (P(TENSOR, FSDP), P(TENSOR, FSDP), P(FSDP, None))
    return jax.shard_map(
        per_device,
        mesh=finer,
        in_specs=placed,
        out_specs=(P(TENSOR, FSDP), P(TENSOR, FSDP), P(FSDP, None)),
        check_vma=False,
    )
```

```python
import functools

import jax
import jax.numpy as jnp
from jax import lax
from jax.experimental import pallas as pl
from jax.experimental.pallas import tpu as pltpu
from jax.sharding import Mesh
from jax.sharding import PartitionSpec as P

ROWS = 4096
COLS = 28672
RANK = 512
FSDP = ("fsdp_0", "fsdp_1")
TENSOR = ("tensor_0", "tensor_1")
R = 512
N = 1792
B = 32
MESH = pl.DeviceIdType.MESH
HIGHEST = lax.Precision.HIGHEST
F32 = jnp.float32
BF16 = jnp.bfloat16
NT = ((1,), (1,))


def mul(a, b, dims=((1,), (0,)), precision=None):
    return lax.dot_general(a, b, (dims, ((), ())), precision=precision, preferred_element_type=F32)


def halves(x):
    high = x.astype(BF16)
    return high, (x - high.astype(F32)).astype(BF16)


def mul3(ah, al, bh, bl, dims=((1,), (0,))):
    return mul(ah, bh, dims) + (mul(ah, bl, dims) + mul(al, bh, dims))


def thirds(x):
    high = x.astype(BF16)
    rest = x - high.astype(F32)
    middle = rest.astype(BF16)
    return high, middle, (rest - middle.astype(F32)).astype(BF16)


def spread(x):
    return jnp.broadcast_to(x, (8, 128))


def factor(block, off):
    n = B // 8
    row = lax.broadcasted_iota(jnp.int32, (8, 128), 0)
    lane = lax.broadcasted_iota(jnp.int32, (8, 128), 1) % B
    rest = [block[8 * h : 8 * h + 8] for h in range(n)]
    inv = [(row + 8 * h == lane).astype(F32) for h in range(n)]
    for base in range(0, B, 16):
        end = base + 16
        col = {m: {h: spread(rest[h][:, off + m : off + m + 1]) for h in range(m // 8, n)} for m in range(base, end)}
        for j in range(base, end):
            g, s = j // 8, j % 8
            r = lax.rsqrt(spread(col[j][g][s : s + 1, :]))
            low = {h: col[j][h] * r for h in range(g, n)}
            top = spread(inv[g][s : s + 1, :]) * r
            inv[g] = jnp.where(row == s, top, inv[g])
            if s < 7:
                inv[g] = inv[g] - jnp.where(row > s, low[g], 0.0) * top
            for h in range(g + 1, n):
                inv[h] = inv[h] - low[h] * top
            for m in range(j + 1, end):
                u = spread(low[m // 8][m % 8 : m % 8 + 1, :])
                for h in range(m // 8, n):
                    col[m][h] = col[m][h] - low[h] * u
            if end < B:
                line = spread(rest[g][s : s + 1, :]) * r
                for h in range(g, n):
                    rest[h] = rest[h] - low[h] * line
    return jnp.concatenate(inv, axis=0)


def paired(x):
    high, middle, low = (part.astype(F32) for part in thirds(x))
    place = lax.broadcasted_iota(jnp.int32, x.shape, 1) // B
    first = jnp.where(place % 2 == 0, high, middle).astype(BF16)
    return first, jnp.where(place == 0, low, high).astype(BF16)[:, : 2 * B]


def stacked(x):
    high, middle, low = thirds(x)
    return jnp.concatenate([high, high, middle, middle], axis=0), jnp.concatenate([high, low], axis=0)


def six(first, second):
    return mul(first[0], second[0]) + mul(first[1], second[1])


def cholesky_step(aug, k):
    r0 = k * B
    r1 = r0 + B
    lo = 128 * (r0 // 128)
    hi = R + lo + 128
    off = r0 - lo
    t = factor(aug[r0:r1, lo : lo + 128], off)
    u = six(paired(t), stacked(aug[r0:r1, lo:hi]))
    aug[r0:r1, R:hi] = u[:, R - lo :]
    if r1 == R:
        return
    high, middle, low = thirds(u)
    over = jnp.concatenate([high, middle, high, middle, low, high], axis=0)
    under = jnp.concatenate([high, high, middle, middle, high, low], axis=0)
    top = r1
    while top < R:
        left = 128 * (top // 128)
        end = r1 + B if top == r1 else left + 128
        if end > top:
            part = mul(over[:, top - lo : end - lo], under[:, left - lo :], ((0,), (0,)))
            aug[top:end, left:hi] = aug[top:end, left:hi] - part
        top = end


def work(
    mom_ref, grad_ref, rf_ref,
    rt_out, mom_out, odh_ref, odl_ref, d_ref,
    mom, grad, rf, bh, bl, rh, rl, lp, left, rsb, ltf, lth, ltl,
    wp, wo, wr, z1, z2, wf, gs, gz, gq, aug, rt, csb,
    in_sem, out_sem,
    ls_send, ls_recv, la_send, la_recv,
    g_send, g_recv, ga_send, ga_recv, gc_send, gc_recv,
    wc_send, wc_recv, wz_send, wz_recv, wd_send, wd_recv,
    cs_send, cs_recv,
):
    z, c = lax.axis_index("tensor_0"), lax.axis_index("tensor_1")
    x, y = lax.axis_index("fsdp_0"), lax.axis_index("fsdp_1")
    me = 4 * x + y
    other_core = {"tensor_1": 1 - c}

    def one(i):
        return i + 1 - 2 * lax.rem(i, 2), lax.rem(lax.rem(i, 2) + lax.div(i, 2), 2)

    def two(i):
        return 3 - i, lax.div(i, 2)

    (xa, xab), (xb, xbb) = one(x), two(x)
    (ya, yab), (yb, ybb) = one(y), two(y)
    (za, zab), (zb, zbb) = one(z), two(z)
    plane = [({"fsdp_0": xa}, xab), ({"fsdp_1": ya}, yab), ({"fsdp_0": xb}, xbb), ({"fsdp_1": yb}, ybb)]
    orders = [plane[p:] + plane[:p] for p in range(4)]
    column = [({"tensor_0": za}, zab), ({"tensor_0": zb}, zbb)]
    zorders = [[column[q % 2], column[1 - q % 2]] for q in range(8)]

    def rows(start, size):
        return pl.ds(pl.multiple_of(start, 8), size)

    def send(src, dst, send_sem, recv_sem, to):
        copy = pltpu.make_async_remote_copy(src, dst, send_sem, recv_sem, device_id=to, device_id_type=MESH)
        copy.start()
        sent.append(copy)
        return copy

    sent = []

    barrier = pltpu.get_barrier_semaphore()
    plane_peers = [
        {"fsdp_0": lax.rem(x + dx, 4), "fsdp_1": lax.rem(y + dy, 4)} for dx in range(4) for dy in range(4) if dx or dy
    ]
    tensor_peers = [
        ({"tensor_0": lax.rem(z + dz, 4), "tensor_1": core}, core)
        for dz in range(4)
        for core in ((c, 1 - c) if dz else (1 - c,))
    ]
    for to in plane_peers + [to for to, _ in tensor_peers]:
        pl.semaphore_signal(barrier, inc=1, device_id=to, device_id_type=MESH)

    cuts = [(0, 512), (512, 1024), (1024, 1536), (1536, N)]
    ins = [[] for _ in range(4)]
    for i, (start, end) in enumerate(cuts):
        s = slice(start, end)
        ins[i].append(pltpu.make_async_copy(rf_ref.at[s], rf.at[s], in_sem.at[3 * i]))
        ins[i].append(pltpu.make_async_copy(mom_ref.at[:, s], mom.at[:, s], in_sem.at[3 * i + 1]))
        ins[i].append(pltpu.make_async_copy(grad_ref.at[:, s], grad.at[:, s], in_sem.at[3 * i + 2]))
    for piece in ins:
        for copy in piece:
            copy.start()

    scatter, gather = {}, {}
    flips = [(1, 0), (0, 1), (1, 1)]

    def quarter(p, stage):
        (to0, bit0), (to1, bit1) = orders[p][2 * stage : 2 * stage + 2]
        peers = []
        for f0, f1 in flips:
            to = {**(to0 if f0 else {}), **(to1 if f1 else {})}
            peers.append((to, 2 * (1 - bit0 if f0 else bit0) + (1 - bit1 if f1 else bit1)))
        return 2 * bit0 + bit1, peers

    quarters = [[quarter(p, stage) for stage in range(2)] for p in range(4)]
    large = [128 * p + 32 * quarters[p][0][0] for p in range(4)]
    small = [large[p] + 8 * quarters[p][1][0] for p in range(4)]

    def scatter_send(h, p, stage):
        base, size, place = (128 * p, 32, 0) if stage == 0 else (large[p], 8, 96)
        for i, (to, index) in enumerate(quarters[p][stage][1]):
            k = 3 * stage + i
            dst = rsb.at[h, p, place + size * i : place + size * i + size]
            src = lp.at[h, rows(base + size * index, size)]
            scatter[h, p, k] = send(src, dst, ls_send.at[h, p, k], ls_recv.at[h, p, k], to)

    def gather_send(h, p, stage):
        part = left.at[h, rows(small[p], 8) if stage else rows(large[p], 32)]
        for i, (to, _) in enumerate(quarters[p][stage][1]):
            k = 3 * stage + i
            gather[h, p, k] = send(part, part, la_send.at[h, p, k], la_recv.at[h, p, k], to)

    def left_step(h, i):
        for p in range(4):
            stage = i if i < 2 else 3 - i
            copies = gather if i >= 2 else scatter
            for k in range(3 * stage, 3 * stage + 3):
                copies[h, p, k].wait_recv()
            if i == 0:
                keep = rows(large[p], 32)
                lp[h, keep, :] = (lp[h, keep, :] + rsb[h, p, :32, :]) + (rsb[h, p, 32:64, :] + rsb[h, p, 64:96, :])
                scatter_send(h, p, 1)
            elif i == 1:
                keep = rows(small[p], 8)
                left[h, keep, :] = (lp[h, keep, :] + rsb[h, p, 96:104, :]) + (rsb[h, p, 104:112, :] + rsb[h, p, 112:, :])
                gather_send(h, p, 1)
            elif i == 2:
                gather_send(h, p, 0)

    for i, (start, end) in enumerate(cuts):
        for copy in ins[i]:
            copy.wait()
        s = slice(start, end)
        rh[s, :256], rl[s, :256] = halves(rf[s, :256])
        bh[:, s], bl[:, s] = halves(mom[:, s] + grad[:, s].astype(F32))
        part = mul3(bh[:, s], bl[:, s], rh[s, :256], rl[s, :256])
        lp[0] = part if i == 0 else lp[0] + part
    pl.semaphore_wait(barrier, 22)
    for p in range(4):
        scatter_send(0, p, 0)
    rh[:, 256:], rl[:, 256:] = halves(rf[:, 256:])
    lp[1] = mul3(bh[...], bl[...], rh[:, 256:], rl[:, 256:])
    for p in range(4):
        scatter_send(1, p, 0)

    places = [[(0, 0), (0, 1), (0, 2), (0, 3), (3, 3)], [(1, 1), (1, 2), (1, 3), (2, 2), (2, 3)]]
    grams = []

    def gram_1():
        mine = jnp.concatenate([ltf[rows(128 * t + 8 * me, 8), :] for t in range(4)], axis=0)
        part = [mul(mine, left[h], precision=HIGHEST) for h in range(2)]
        for core in range(2):
            for i, (t, n) in enumerate(places[core]):
                gs[core, i] = part[n // 2][8 * t : 8 * t + 8, 128 * (n % 2) : 128 * (n % 2) + 128]
        slot = 2 * z + c
        for i, (to, core) in enumerate(tensor_peers):
            grams.append(send(gs.at[core], gz.at[slot], g_send.at[i], g_recv.at[i], to))
        gz[slot] = gs[c]

    gathers = []

    def gram_2():
        for copy in grams:
            copy.wait_recv()
        total = gz[0]
        for i in range(1, 8):
            total = total + gz[i]
        gq[c, me] = total
        for i, to in enumerate(plane_peers):
            part = gq.at[c, me]
            gathers.append(send(part, part, ga_send.at[i], ga_recv.at[i], to))

    def gram_3():
        for copy in gathers:
            copy.wait_recv()
        grams.append(send(gq.at[c], gq.at[c], gc_send, gc_recv, other_core))

    def gram_4():
        grams[-1].wait_recv()
        for core in range(2):
            for i, (t, n) in enumerate(places[core]):
                for j in range(16):
                    aug[128 * t + 8 * j : 128 * t + 8 * j + 8, 128 * n : 128 * n + 128] = gq[core, j, i]
        row = lax.broadcasted_iota(jnp.int32, (R, R), 0)
        aug[:, R:] = (row == lax.broadcasted_iota(jnp.int32, (R, R), 1)).astype(F32)

    wcore, wscatter, wgather = {}, {}, {}

    def turn(h):
        half = slice(256 * h, 256 * h + 256)
        ltf[half, :] = left[h].T
        lth[half, :], ltl[half, :] = halves(ltf[half, :])

    def w_other(h):
        s = rows(256 * h + 128 * (1 - c), 128)
        wp[h] = mul3(lth[s, :], ltl[s, :], bh[...], bl[...])
        for q in range(4):
            part = slice(32 * q, 32 * q + 32)
            k = 4 * h + q
            wcore[k] = send(wp.at[h, part], wr.at[h, part], wc_send.at[k], wc_recv.at[k], other_core)

    def w_own(h):
        s = rows(256 * h + 128 * c, 128)
        wo[h] = mul3(lth[s, :], ltl[s, :], bh[...], bl[...])

    woff = []
    for q in range(8):
        o0 = 32 * (q % 4)
        o1 = o0 + 16 * zorders[q][0][1]
        woff.append((o0, o1, o1 + 8 * zorders[q][1][1]))

    def w_send(q, s, buf):
        to, bit = zorders[q][s]
        size = 16 >> s
        src = wo.at[q // 4, rows(woff[q][s] + (1 - bit) * size, size)]
        wscatter[q, s] = send(src, buf.at[q], wz_send.at[q, s], wz_recv.at[q, s], to)

    def w_1(q):
        wcore[q].wait_recv()
        part = slice(woff[q][0], woff[q][0] + 32)
        wo[q // 4, part, :] = wo[q // 4, part, :] + wr[q // 4, part, :]
        w_send(q, 0, z1)

    def w_2(q):
        wscatter[q, 0].wait_recv()
        keep = rows(woff[q][1], 16)
        wo[q // 4, keep, :] = wo[q // 4, keep, :] + z1[q]
        w_send(q, 1, z2)

    def w_gather(q, i, start, size, to):
        part = wf.at[rows(256 * (q // 4) + 128 * c + start, size)]
        wgather[q, i] = send(part, part, wd_send.at[q, i], wd_recv.at[q, i], to)

    def w_3(q):
        wscatter[q, 1].wait_recv()
        own = rows(256 * (q // 4) + 128 * c + woff[q][2], 8)
        wf[own, :] = wo[q // 4, rows(woff[q][2], 8), :] + z2[q]
        w_gather(q, 0, woff[q][2], 8, zorders[q][1][0])

    def w_4(q):
        wgather[q, 0].wait_recv()
        w_gather(q, 1, woff[q][1], 16, zorders[q][0][0])

    def w_5(q):
        wgather[q, 1].wait_recv()
        w_gather(q, 2, woff[q][0], 32, other_core)

    def pairs(step, *firsts):
        return [(step, q) for first in firsts for q in (first, first + 1)]

    for i in range(3):
        left_step(0, i)
        left_step(1, i)
    left_step(0, 3)
    turn(0)
    w_other(0)
    left_step(1, 3)
    turn(1)
    gram_1()
    w_own(0)
    for step, q in pairs(w_1, 0, 2):
        step(q)
    w_other(1)
    w_own(1)
    for step, q in pairs(w_1, 4, 6):
        step(q)
    gram_2()
    for step, q in pairs(w_2, 0, 2):
        step(q)
    gram_3()
    gram_4()
    between = {
        1: pairs(w_2, 4, 6),
        2: pairs(w_3, 0, 2),
        4: pairs(w_3, 4, 6),
        6: pairs(w_4, 0, 2),
        8: pairs(w_4, 4, 6),
        12: pairs(w_5, 0),
        13: pairs(w_5, 2),
        15: pairs(w_5, 4),
    }
    for k in range(R // B):
        cholesky_step(aug, k)
        for step, q in between.get(k, []):
            step(q)

    for q in range(4):
        wgather[q, 2].wait_recv()
    for n in range(0, N, 256):
        if n == 1024:
            w_5(6)
        ih, il = halves(aug[:, R : R + 256])
        wh, wl = halves(wf[:256, n : n + 256])
        rt[:, n : n + 256] = mul3(ih, il, wh, wl)
    w_5(7)
    for q in range(4, 8):
        wgather[q, 2].wait_recv()
    ih, il = halves(aug[256:, R + 256 :])
    for n in range(0, N, 256):
        wh, wl = halves(wf[256:, n : n + 256])
        rt[256:, n : n + 256] = rt[256:, n : n + 256] + mul3(ih, il, wh, wl)
    sums = jnp.zeros((R, 128), F32)
    for n in range(0, N, 128):
        sums = sums + rt[:, n : n + 128] * rt[:, n : n + 128]
    line = [jnp.sum(sums[128 * i : 128 * i + 128].T, axis=0, keepdims=True) for i in range(4)]
    csb[me] = jnp.concatenate(line + [jnp.zeros((4, 128), F32)], axis=0)
    squares = []
    for i, to in enumerate(plane_peers):
        squares.append(send(csb.at[me], csb.at[me], cs_send.at[i], cs_recv.at[i], to))
    outs = [pltpu.make_async_copy(rt, rt_out, out_sem.at[0])]
    outs[0].start()
    lh, ll = halves(jnp.concatenate([left[0], left[1]], axis=1))
    ih, il = halves(aug[:, R:])
    ortho = mul3(lh, ll, ih, il, NT)
    small_ortho = (ortho * 0.05).astype(BF16)
    for start, end in ((0, 768), (768, N)):
        s = slice(start, end)
        for n in range(start, end, 256):
            m = slice(n, n + 256)
            mom[:, m] = mom[:, m] + grad[:, m].astype(F32) - mul(small_ortho, rt[:, m].astype(BF16))
        outs.append(pltpu.make_async_copy(mom.at[:, s], mom_out.at[:, s], out_sem.at[len(outs)]))
        outs[-1].start()
    for copy in squares:
        copy.wait_recv()
    total = csb[0]
    for i in range(1, 16):
        total = total + csb[i]
    norm = 1.0 / jnp.sqrt(total + 1e-06)
    d = jnp.concatenate([norm[i : i + 1, :] for i in range(4)], axis=1)
    d_ref[...] = jnp.broadcast_to(d, (8, R))
    scale = (ROWS * COLS / RANK) ** 0.5
    odh_ref[...], odl_ref[...] = halves(ortho * (d * scale))
    for copy in outs:
        copy.wait()
    for copy in sent:
        copy.wait_send()


def finish(mom, rt, odh, odl, d, new_mom, update, new_right):
    right = rt[...]
    rh, rl = halves(right)
    update[...] = mul3(odh[...], odl[...], rh, rl)
    new_mom[...] = mom[...]
    new_right[...] = right.T * d[0:1, :]


def per_device(momentum, gradient, right_factor):
    vmem, dma, anywhere = pltpu.VMEM, pltpu.SemaphoreType.DMA, pl.BlockSpec(memory_space=pl.ANY)
    inside = pl.BlockSpec(memory_space=pltpu.VMEM)
    rt, mom, odh, odl, d = pl.pallas_call(
        work,
        out_shape=[
            jax.ShapeDtypeStruct((R, N), F32),
            jax.ShapeDtypeStruct((R, N), F32),
            jax.ShapeDtypeStruct((R, RANK), BF16),
            jax.ShapeDtypeStruct((R, RANK), BF16),
            jax.ShapeDtypeStruct((8, RANK), F32),
        ],
        in_specs=[anywhere] * 3,
        out_specs=[anywhere, anywhere, inside, inside, inside],
        scratch_shapes=[
            vmem((R, N), F32), vmem((R, N), BF16), vmem((N, RANK), F32),
            vmem((R, N), BF16), vmem((R, N), BF16), vmem((N, RANK), BF16), vmem((N, RANK), BF16),
            vmem((2, R, 256), F32), vmem((2, R, 256), F32), vmem((2, 4, 120, 256), F32),
            vmem((RANK, R), F32), vmem((RANK, R), BF16), vmem((RANK, R), BF16),
            vmem((2, 128, N), F32), vmem((2, 128, N), F32), vmem((2, 128, N), F32),
            vmem((8, 16, N), F32), vmem((8, 8, N), F32), vmem((RANK, N), F32),
            vmem((2, 5, 8, 128), F32), vmem((8, 5, 8, 128), F32), vmem((2, 16, 5, 8, 128), F32),
            vmem((RANK, 2 * RANK), F32), vmem((RANK, N), F32), vmem((16, 8, 128), F32),
            dma((12,)), dma((3,)),
            dma((2, 4, 6)), dma((2, 4, 6)), dma((2, 4, 6)), dma((2, 4, 6)),
            dma((7,)), dma((7,)), dma((15,)), dma((15,)), dma, dma,
            dma((8,)), dma((8,)), dma((8, 2)), dma((8, 2)), dma((8, 3)), dma((8, 3)),
            dma((15,)), dma((15,)),
        ],
        compiler_params=pltpu.CompilerParams(
            collective_id=0, has_side_effects=True, vmem_limit_bytes=62 << 20
        ),
        name="dion",
    )(momentum, gradient, right_factor)
    wide = 896
    tall = pl.BlockSpec((R, wide), lambda i: (0, i))
    whole = pl.BlockSpec((R, RANK), lambda i: (0, 0))
    return pl.pallas_call(
        finish,
        out_shape=[
            jax.ShapeDtypeStruct((R, N), F32),
            jax.ShapeDtypeStruct((R, N), F32),
            jax.ShapeDtypeStruct((N, RANK), F32),
        ],
        grid=(N // wide,),
        in_specs=[tall, tall, whole, whole, pl.BlockSpec((8, RANK), lambda i: (0, 0))],
        out_specs=[tall, tall, pl.BlockSpec((wide, RANK), lambda i: (i, 0))],
        compiler_params=pltpu.CompilerParams(vmem_limit_bytes=56 << 20),
        name="finish",
    )(mom, rt, odh, odl, d)


def solution(mesh):
    finer = Mesh(mesh.devices.reshape(4, 2, 4, 4), ("tensor_0", "tensor_1", "fsdp_0", "fsdp_1"))
    placed = (P(TENSOR, FSDP), P(TENSOR, FSDP), P(FSDP, None))
    return jax.shard_map(
        per_device,
        mesh=finer,
        in_specs=placed,
        out_specs=(P(TENSOR, FSDP), P(TENSOR, FSDP), P(FSDP, None)),
        check_vma=False,
    )
```

```python
import functools

import jax
import jax.numpy as jnp
from jax import lax
from jax.experimental import pallas as pl
from jax.experimental.pallas import tpu as pltpu
from jax.sharding import Mesh
from jax.sharding import PartitionSpec as P

ROWS = 4096
COLS = 28672
RANK = 512
FSDP = ("fsdp_0", "fsdp_1")
TENSOR = ("tensor_0", "tensor_1")
R = 512
N = 1792
B = 32
MESH = pl.DeviceIdType.MESH
HIGHEST = lax.Precision.HIGHEST
F32 = jnp.float32
BF16 = jnp.bfloat16
NT = ((1,), (1,))


def mul(a, b, dims=((1,), (0,)), precision=None):
    return lax.dot_general(a, b, (dims, ((), ())), precision=precision, preferred_element_type=F32)


def halves(x):
    high = x.astype(BF16)
    return high, (x - high.astype(F32)).astype(BF16)


def mul3(ah, al, bh, bl, dims=((1,), (0,))):
    return mul(ah, bh, dims) + (mul(ah, bl, dims) + mul(al, bh, dims))


def thirds(x):
    high = x.astype(BF16)
    rest = x - high.astype(F32)
    middle = rest.astype(BF16)
    return high, middle, (rest - middle.astype(F32)).astype(BF16)


def spread(x):
    return jnp.broadcast_to(x, (8, 128))


def factor(block, off):
    n = B // 8
    row = lax.broadcasted_iota(jnp.int32, (8, 128), 0)
    lane = lax.broadcasted_iota(jnp.int32, (8, 128), 1) % B
    rest = [block[8 * h : 8 * h + 8] for h in range(n)]
    inv = [(row + 8 * h == lane).astype(F32) for h in range(n)]
    for base in range(0, B, 16):
        end = base + 16
        col = {m: {h: spread(rest[h][:, off + m : off + m + 1]) for h in range(m // 8, n)} for m in range(base, end)}
        for j in range(base, end):
            g, s = j // 8, j % 8
            r = lax.rsqrt(spread(col[j][g][s : s + 1, :]))
            low = {h: col[j][h] * r for h in range(g, n)}
            top = spread(inv[g][s : s + 1, :]) * r
            inv[g] = jnp.where(row == s, top, inv[g])
            if s < 7:
                inv[g] = inv[g] - jnp.where(row > s, low[g], 0.0) * top
            for h in range(g + 1, n):
                inv[h] = inv[h] - low[h] * top
            for m in range(j + 1, end):
                u = spread(low[m // 8][m % 8 : m % 8 + 1, :])
                for h in range(m // 8, n):
                    col[m][h] = col[m][h] - low[h] * u
            if end < B:
                line = spread(rest[g][s : s + 1, :]) * r
                for h in range(g, n):
                    rest[h] = rest[h] - low[h] * line
    return jnp.concatenate(inv, axis=0)


def paired(x):
    high, middle, low = (part.astype(F32) for part in thirds(x))
    place = lax.broadcasted_iota(jnp.int32, x.shape, 1) // B
    first = jnp.where(place % 2 == 0, high, middle).astype(BF16)
    return first, jnp.where(place == 0, low, high).astype(BF16)[:, : 2 * B]


def stacked(x):
    high, middle, low = thirds(x)
    return jnp.concatenate([high, high, middle, middle], axis=0), jnp.concatenate([high, low], axis=0)


def six(first, second):
    return mul(first[0], second[0]) + mul(first[1], second[1])


def cholesky_step(aug, k):
    r0 = k * B
    r1 = r0 + B
    lo = 128 * (r0 // 128)
    hi = R + lo + 128
    off = r0 - lo
    t = factor(aug[r0:r1, lo : lo + 128], off)
    u = six(paired(t), stacked(aug[r0:r1, lo:hi]))
    aug[r0:r1, R:hi] = u[:, R - lo :]
    if r1 == R:
        return
    high, middle, low = thirds(u)
    over = jnp.concatenate([high, middle, high, middle, low, high], axis=0)
    under = jnp.concatenate([high, high, middle, middle, high, low], axis=0)
    top = r1
    while top < R:
        left = 128 * (top // 128)
        end = r1 + B if top == r1 else left + 128
        if end > top:
            part = mul(over[:, top - lo : end - lo], under[:, left - lo :], ((0,), (0,)))
            aug[top:end, left:hi] = aug[top:end, left:hi] - part
        top = end


def work(
    mom_ref, grad_ref, rf_ref,
    rt_out, mom_out, odh_ref, odl_ref, d_ref,
    mom, grad, rf, bh, bl, rh, rl, lp, left, rsb, ltf, lth, ltl,
    wp, wo, wr, z1, z2, wf, gs, gz, gq, aug, rt, csb,
    in_sem, out_sem,
    ls_send, ls_recv, la_send, la_recv,
    g_send, g_recv, ga_send, ga_recv, gc_send, gc_recv,
    wc_send, wc_recv, wz_send, wz_recv, wd_send, wd_recv,
    cs_send, cs_recv,
):
    z, c = lax.axis_index("tensor_0"), lax.axis_index("tensor_1")
    x, y = lax.axis_index("fsdp_0"), lax.axis_index("fsdp_1")
    me = 4 * x + y
    other_core = {"tensor_1": 1 - c}

    def one(i):
        return i + 1 - 2 * lax.rem(i, 2), lax.rem(lax.rem(i, 2) + lax.div(i, 2), 2)

    def two(i):
        return 3 - i, lax.div(i, 2)

    (xa, xab), (xb, xbb) = one(x), two(x)
    (ya, yab), (yb, ybb) = one(y), two(y)
    (za, zab), (zb, zbb) = one(z), two(z)
    plane = [({"fsdp_0": xa}, xab), ({"fsdp_1": ya}, yab), ({"fsdp_0": xb}, xbb), ({"fsdp_1": yb}, ybb)]
    orders = [plane[p:] + plane[:p] for p in range(4)]
    column = [({"tensor_0": za}, zab), ({"tensor_0": zb}, zbb)]
    zorders = [[column[q % 2], column[1 - q % 2]] for q in range(8)]

    def rows(start, size):
        return pl.ds(pl.multiple_of(start, 8), size)

    def send(src, dst, send_sem, recv_sem, to):
        copy = pltpu.make_async_remote_copy(src, dst, send_sem, recv_sem, device_id=to, device_id_type=MESH)
        copy.start()
        sent.append(copy)
        return copy

    sent = []

    def drain(count):
        for copy in sent[:count]:
            copy.wait_send()
        del sent[:count]

    barrier = pltpu.get_barrier_semaphore()
    plane_peers = [
        {"fsdp_0": lax.rem(x + dx, 4), "fsdp_1": lax.rem(y + dy, 4)} for dx in range(4) for dy in range(4) if dx or dy
    ]
    tensor_peers = [
        ({"tensor_0": lax.rem(z + dz, 4), "tensor_1": core}, core)
        for dz in range(4)
        for core in ((c, 1 - c) if dz else (1 - c,))
    ]
    for to in plane_peers + [to for to, _ in tensor_peers]:
        pl.semaphore_signal(barrier, inc=1, device_id=to, device_id_type=MESH)

    cuts = [(0, 512), (512, 1024), (1024, 1536), (1536, N)]
    ins = [[] for _ in range(4)]
    for i, (start, end) in enumerate(cuts):
        s = slice(start, end)
        ins[i].append(pltpu.make_async_copy(rf_ref.at[s], rf.at[s], in_sem.at[3 * i]))
        ins[i].append(pltpu.make_async_copy(mom_ref.at[:, s], mom.at[:, s], in_sem.at[3 * i + 1]))
        ins[i].append(pltpu.make_async_copy(grad_ref.at[:, s], grad.at[:, s], in_sem.at[3 * i + 2]))
    for piece in ins:
        for copy in piece:
            copy.start()

    scatter, gather = {}, {}
    flips = [(1, 0), (0, 1), (1, 1)]

    def quarter(p, stage):
        (to0, bit0), (to1, bit1) = orders[p][2 * stage : 2 * stage + 2]
        peers = []
        for f0, f1 in flips:
            to = {**(to0 if f0 else {}), **(to1 if f1 else {})}
            peers.append((to, 2 * (1 - bit0 if f0 else bit0) + (1 - bit1 if f1 else bit1)))
        return 2 * bit0 + bit1, peers

    quarters = [[quarter(p, stage) for stage in range(2)] for p in range(4)]
    large = [128 * p + 32 * quarters[p][0][0] for p in range(4)]
    small = [large[p] + 8 * quarters[p][1][0] for p in range(4)]

    def scatter_send(h, p, stage):
        base, size, place = (128 * p, 32, 0) if stage == 0 else (large[p], 8, 96)
        for i, (to, index) in enumerate(quarters[p][stage][1]):
            k = 3 * stage + i
            dst = rsb.at[h, p, place + size * i : place + size * i + size]
            src = lp.at[h, rows(base + size * index, size)]
            scatter[h, p, k] = send(src, dst, ls_send.at[h, p, k], ls_recv.at[h, p, k], to)

    def gather_send(h, p, stage):
        part = left.at[h, rows(small[p], 8) if stage else rows(large[p], 32)]
        for i, (to, _) in enumerate(quarters[p][stage][1]):
            k = 3 * stage + i
            gather[h, p, k] = send(part, part, la_send.at[h, p, k], la_recv.at[h, p, k], to)

    def left_step(h, i):
        for p in range(4):
            stage = i if i < 2 else 3 - i
            copies = gather if i >= 2 else scatter
            for k in range(3 * stage, 3 * stage + 3):
                copies[h, p, k].wait_recv()
            if i == 0:
                keep = rows(large[p], 32)
                lp[h, keep, :] = (lp[h, keep, :] + rsb[h, p, :32, :]) + (rsb[h, p, 32:64, :] + rsb[h, p, 64:96, :])
                scatter_send(h, p, 1)
            elif i == 1:
                keep = rows(small[p], 8)
                left[h, keep, :] = (lp[h, keep, :] + rsb[h, p, 96:104, :]) + (rsb[h, p, 104:112, :] + rsb[h, p, 112:, :])
                gather_send(h, p, 1)
            elif i == 2:
                gather_send(h, p, 0)

    for i, (start, end) in enumerate(cuts):
        for copy in ins[i]:
            copy.wait()
        s = slice(start, end)
        rh[s, :256], rl[s, :256] = halves(rf[s, :256])
        bh[:, s], bl[:, s] = halves(mom[:, s] + grad[:, s].astype(F32))
        part = mul3(bh[:, s], bl[:, s], rh[s, :256], rl[s, :256])
        lp[0] = part if i == 0 else lp[0] + part
    pl.semaphore_wait(barrier, 22)
    for p in range(4):
        scatter_send(0, p, 0)
    rh[:, 256:], rl[:, 256:] = halves(rf[:, 256:])
    lp[1] = mul3(bh[...], bl[...], rh[:, 256:], rl[:, 256:])
    for p in range(4):
        scatter_send(1, p, 0)

    places = [[(0, 0), (0, 1), (0, 2), (0, 3), (3, 3)], [(1, 1), (1, 2), (1, 3), (2, 2), (2, 3)]]
    grams = []

    def gram_1():
        mine = jnp.concatenate([ltf[rows(128 * t + 8 * me, 8), :] for t in range(4)], axis=0)
        part = [mul(mine, left[h], precision=HIGHEST) for h in range(2)]
        for core in range(2):
            for i, (t, n) in enumerate(places[core]):
                gs[core, i] = part[n // 2][8 * t : 8 * t + 8, 128 * (n % 2) : 128 * (n % 2) + 128]
        slot = 2 * z + c
        for i, (to, core) in enumerate(tensor_peers):
            grams.append(send(gs.at[core], gz.at[slot], g_send.at[i], g_recv.at[i], to))
        gz[slot] = gs[c]

    gathers = []

    def gram_2():
        for copy in grams:
            copy.wait_recv()
        total = gz[0]
        for i in range(1, 8):
            total = total + gz[i]
        gq[c, me] = total
        for i, to in enumerate(plane_peers):
            part = gq.at[c, me]
            gathers.append(send(part, part, ga_send.at[i], ga_recv.at[i], to))

    def gram_3():
        for copy in gathers:
            copy.wait_recv()
        grams.append(send(gq.at[c], gq.at[c], gc_send, gc_recv, other_core))

    def gram_4():
        grams[-1].wait_recv()
        for core in range(2):
            for i, (t, n) in enumerate(places[core]):
                for j in range(16):
                    aug[128 * t + 8 * j : 128 * t + 8 * j + 8, 128 * n : 128 * n + 128] = gq[core, j, i]
        row = lax.broadcasted_iota(jnp.int32, (R, R), 0)
        aug[:, R:] = (row == lax.broadcasted_iota(jnp.int32, (R, R), 1)).astype(F32)

    wcore, wscatter, wgather = {}, {}, {}

    def turn(h):
        half = slice(256 * h, 256 * h + 256)
        ltf[half, :] = left[h].T
        lth[half, :], ltl[half, :] = halves(ltf[half, :])

    def w_other(h):
        s = rows(256 * h + 128 * (1 - c), 128)
        wp[h] = mul3(lth[s, :], ltl[s, :], bh[...], bl[...])
        for q in range(4):
            part = slice(32 * q, 32 * q + 32)
            k = 4 * h + q
            wcore[k] = send(wp.at[h, part], wr.at[h, part], wc_send.at[k], wc_recv.at[k], other_core)

    def w_own(h):
        s = rows(256 * h + 128 * c, 128)
        wo[h] = mul3(lth[s, :], ltl[s, :], bh[...], bl[...])

    woff = []
    for q in range(8):
        o0 = 32 * (q % 4)
        o1 = o0 + 16 * zorders[q][0][1]
        woff.append((o0, o1, o1 + 8 * zorders[q][1][1]))

    def w_send(q, s, buf):
        to, bit = zorders[q][s]
        size = 16 >> s
        src = wo.at[q // 4, rows(woff[q][s] + (1 - bit) * size, size)]
        wscatter[q, s] = send(src, buf.at[q], wz_send.at[q, s], wz_recv.at[q, s], to)

    def w_1(q):
        wcore[q].wait_recv()
        part = slice(woff[q][0], woff[q][0] + 32)
        wo[q // 4, part, :] = wo[q // 4, part, :] + wr[q // 4, part, :]
        w_send(q, 0, z1)

    def w_2(q):
        wscatter[q, 0].wait_recv()
        keep = rows(woff[q][1], 16)
        wo[q // 4, keep, :] = wo[q // 4, keep, :] + z1[q]
        w_send(q, 1, z2)

    def w_gather(q, i, start, size, to):
        part = wf.at[rows(256 * (q // 4) + 128 * c + start, size)]
        wgather[q, i] = send(part, part, wd_send.at[q, i], wd_recv.at[q, i], to)

    def w_3(q):
        wscatter[q, 1].wait_recv()
        own = rows(256 * (q // 4) + 128 * c + woff[q][2], 8)
        wf[own, :] = wo[q // 4, rows(woff[q][2], 8), :] + z2[q]
        w_gather(q, 0, woff[q][2], 8, zorders[q][1][0])

    def w_4(q):
        wgather[q, 0].wait_recv()
        w_gather(q, 1, woff[q][1], 16, zorders[q][0][0])

    def w_5(q):
        wgather[q, 1].wait_recv()
        w_gather(q, 2, woff[q][0], 32, other_core)

    def pairs(step, *firsts):
        return [(step, q) for first in firsts for q in (first, first + 1)]

    for i in range(3):
        left_step(0, i)
        left_step(1, i)
    left_step(0, 3)
    turn(0)
    w_other(0)
    left_step(1, 3)
    turn(1)
    gram_1()
    w_own(0)
    for step, q in pairs(w_1, 0, 2):
        step(q)
    w_other(1)
    w_own(1)
    for step, q in pairs(w_1, 4, 6):
        step(q)
    drain(96)
    gram_2()
    for step, q in pairs(w_2, 0, 2):
        step(q)
    gram_3()
    gram_4()
    between = {
        1: pairs(w_2, 4, 6),
        2: pairs(w_3, 0, 2),
        4: pairs(w_3, 4, 6),
        6: pairs(w_4, 0, 2),
        8: pairs(w_4, 4, 6),
        12: pairs(w_5, 0),
        13: pairs(w_5, 2),
        15: pairs(w_5, 4),
    }
    for k in range(R // B):
        cholesky_step(aug, k)
        for step, q in between.get(k, []):
            step(q)

    for q in range(4):
        wgather[q, 2].wait_recv()
    for n in range(0, N, 256):
        if n == 1024:
            w_5(6)
        ih, il = halves(aug[:, R : R + 256])
        wh, wl = halves(wf[:256, n : n + 256])
        rt[:, n : n + 256] = mul3(ih, il, wh, wl)
    w_5(7)

    def squared(top):
        sums = jnp.zeros((256, 128), F32)
        for n in range(0, N, 128):
            sums = sums + rt[top : top + 256, n : n + 128] * rt[top : top + 256, n : n + 128]
        return [jnp.sum(sums[i : i + 128].T, axis=0, keepdims=True) for i in (0, 128)]

    line = squared(0)
    for q in range(4, 8):
        wgather[q, 2].wait_recv()
    ih, il = halves(aug[256:, R + 256 :])
    for n in range(0, N, 256):
        wh, wl = halves(wf[256:, n : n + 256])
        rt[256:, n : n + 256] = rt[256:, n : n + 256] + mul3(ih, il, wh, wl)

    line += squared(256)
    csb[me] = jnp.concatenate(line + [jnp.zeros((4, 128), F32)], axis=0)
    squares = []
    for i, to in enumerate(plane_peers):
        squares.append(send(csb.at[me], csb.at[me], cs_send.at[i], cs_recv.at[i], to))
    outs = [pltpu.make_async_copy(rt, rt_out, out_sem.at[0])]
    outs[0].start()
    lh, ll = halves(jnp.concatenate([left[0], left[1]], axis=1))
    ih, il = halves(aug[:, R:])
    ortho = mul3(lh, ll, ih, il, NT)
    small_ortho = (ortho * 0.05).astype(BF16)
    for start, end in ((0, 768), (768, N)):
        s = slice(start, end)
        for n in range(start, end, 256):
            m = slice(n, n + 256)
            mom[:, m] = mom[:, m] + grad[:, m].astype(F32) - mul(small_ortho, rt[:, m].astype(BF16))
        outs.append(pltpu.make_async_copy(mom.at[:, s], mom_out.at[:, s], out_sem.at[len(outs)]))
        outs[-1].start()
    drain(len(sent) - len(squares))
    for copy in squares:
        copy.wait_recv()
    total = csb[0]
    for i in range(1, 16):
        total = total + csb[i]
    norm = 1.0 / jnp.sqrt(total + 1e-06)
    d = jnp.concatenate([norm[i : i + 1, :] for i in range(4)], axis=1)
    d_ref[...] = jnp.broadcast_to(d, (8, R))
    scale = (ROWS * COLS / RANK) ** 0.5
    odh_ref[...], odl_ref[...] = halves(ortho * (d * scale))
    for copy in outs:
        copy.wait()
    drain(len(sent))


def finish(mom, rt, odh, odl, d, new_mom, update, new_right):
    right = rt[...]
    rh, rl = halves(right)
    update[...] = mul3(odh[...], odl[...], rh, rl)
    new_mom[...] = mom[...]
    new_right[...] = right.T * d[0:1, :]


def per_device(momentum, gradient, right_factor):
    vmem, dma, anywhere = pltpu.VMEM, pltpu.SemaphoreType.DMA, pl.BlockSpec(memory_space=pl.ANY)
    inside = pl.BlockSpec(memory_space=pltpu.VMEM)
    rt, mom, odh, odl, d = pl.pallas_call(
        work,
        out_shape=[
            jax.ShapeDtypeStruct((R, N), F32),
            jax.ShapeDtypeStruct((R, N), F32),
            jax.ShapeDtypeStruct((R, RANK), BF16),
            jax.ShapeDtypeStruct((R, RANK), BF16),
            jax.ShapeDtypeStruct((8, RANK), F32),
        ],
        in_specs=[anywhere] * 3,
        out_specs=[anywhere, anywhere, inside, inside, inside],
        scratch_shapes=[
            vmem((R, N), F32), vmem((R, N), BF16), vmem((N, RANK), F32),
            vmem((R, N), BF16), vmem((R, N), BF16), vmem((N, RANK), BF16), vmem((N, RANK), BF16),
            vmem((2, R, 256), F32), vmem((2, R, 256), F32), vmem((2, 4, 120, 256), F32),
            vmem((RANK, R), F32), vmem((RANK, R), BF16), vmem((RANK, R), BF16),
            vmem((2, 128, N), F32), vmem((2, 128, N), F32), vmem((2, 128, N), F32),
            vmem((8, 16, N), F32), vmem((8, 8, N), F32), vmem((RANK, N), F32),
            vmem((2, 5, 8, 128), F32), vmem((8, 5, 8, 128), F32), vmem((2, 16, 5, 8, 128), F32),
            vmem((RANK, 2 * RANK), F32), vmem((RANK, N), F32), vmem((16, 8, 128), F32),
            dma((12,)), dma((3,)),
            dma((2, 4, 6)), dma((2, 4, 6)), dma((2, 4, 6)), dma((2, 4, 6)),
            dma((7,)), dma((7,)), dma((15,)), dma((15,)), dma, dma,
            dma((8,)), dma((8,)), dma((8, 2)), dma((8, 2)), dma((8, 3)), dma((8, 3)),
            dma((15,)), dma((15,)),
        ],
        compiler_params=pltpu.CompilerParams(
            collective_id=0, has_side_effects=True, vmem_limit_bytes=62 << 20
        ),
        name="dion",
    )(momentum, gradient, right_factor)
    wide = 896
    tall = pl.BlockSpec((R, wide), lambda i: (0, i))
    whole = pl.BlockSpec((R, RANK), lambda i: (0, 0))
    return pl.pallas_call(
        finish,
        out_shape=[
            jax.ShapeDtypeStruct((R, N), F32),
            jax.ShapeDtypeStruct((R, N), F32),
            jax.ShapeDtypeStruct((N, RANK), F32),
        ],
        grid=(N // wide,),
        in_specs=[tall, tall, whole, whole, pl.BlockSpec((8, RANK), lambda i: (0, 0))],
        out_specs=[tall, tall, pl.BlockSpec((wide, RANK), lambda i: (i, 0))],
        compiler_params=pltpu.CompilerParams(vmem_limit_bytes=56 << 20),
        name="finish",
    )(mom, rt, odh, odl, d)


def solution(mesh):
    finer = Mesh(mesh.devices.reshape(4, 2, 4, 4), ("tensor_0", "tensor_1", "fsdp_0", "fsdp_1"))
    placed = (P(TENSOR, FSDP), P(TENSOR, FSDP), P(FSDP, None))
    return jax.shard_map(
        per_device,
        mesh=finer,
        in_specs=placed,
        out_specs=(P(TENSOR, FSDP), P(TENSOR, FSDP), P(FSDP, None)),
        check_vma=False,
    )
```
